512 devices in a mesh: dp: 4 (over x), ctx: 16 (over y_hi, z), tp: 8 (over y_lo, core).
Axes of the slice: x: 4, y: 8 (y_hi: 2, y_lo: 4; y = y_hi * 4 + y_lo), z: 8, core: 2. Of those that a mesh axis runs over, the one named last changes fastest.
Arguments:
- xbc: bfloat16 [8192, 12288], P(('dp', 'ctx'), 'tp'), parts along dimension 0, may hold values from -6 to 6
- gate_in: bfloat16 [8192, 8192], P(('dp', 'ctx'), 'tp'), parts along dimension 0, may hold values from -6 to 6
- dt_raw: float32 [128, 8192], P('tp', ('dp', 'ctx')), parts along dimension 1, may hold values from -2 to 13.2
- dt_bias: float32 [512], P(('dp', 'tp')), parts along dimension 0, may hold values from -13 to -3
- a_log: float32 [128], P('tp'), may hold values from -0.7 to 0
- conv_weight: float32 [4, 12288], P(None, 'tp'), may hold values from -3 to 3
- conv_bias: float32 [12288], P('tp'), may hold values from -3 to 3
- skip_weight: float32 [128], P('tp'), may hold values from 0.5 to 1.5
- norm_gain: float32 [8192], P('tp'), may hold values from 0.5 to 1.5
- queries: bfloat16 [8192, 8192], P(('dp', 'ctx'), 'tp'), parts along dimension 0, may hold values from -10 to 10
- keys: bfloat16 [8192, 1024], P(('dp', 'ctx'), 'tp'), parts along dimension 0, may hold values from -6 to 6
- values: bfloat16 [8192, 1024], P(('dp', 'ctx'), 'tp'), parts along dimension 0, may hold values from -6 to 6
Outputs:
- mamba_out: bfloat16 [8192, 8192], P(('dp', 'ctx'), 'tp'), parts along dimension 0
- attn_out: bfloat16 [8192, 8192], P(('dp', 'ctx'), 'tp'), parts along dimension 0
The draws below stay inside these ranges and needn't reach their ends.
There are 4 independent parts, one for each index of `dp`. The reference program is written for one: setup_inputs(seed, part) draws one part's arguments, and reference() takes and returns one part's arrays. A program takes and returns all parts, laid end to end along the dimension named above; an argument that names none is the same for every part. Nothing has to cross between parts.
All inputs are finite; a program needn't handle non-finite values.
Results may differ from the reference program's by a relative error of at most 0.0047.
Values may be sent and summed in bfloat16 or wider, within the bound.
No kernel may reach another device: no remote copies, remote signals or barrier semaphores. Data moves between devices by JAX's collectives and lax.ppermute only.
A program may use at most 64 MiB of HBM per device.

```python
import math
import jax
import jax.numpy as jnp
from jax import lax

MAMBA_HEAD_COUNT = 128
SSM_HEAD_DIM = 64
SSM_STATE = 256
SSM_GROUPS = 8
CONV_WIDTH = 4
SPAN_LEN = 128
QUERY_HEADS = 64
KEY_HEADS = 8
KEY_DIM = 128
SEQUENCE_LENGTH = 2048
N_TP = 8


pulse_count = 6


def rate_pieces(key):
    key_bias, key_rough, key_location, key_raise, key_steady, key_steady_bias, key_target = jax.random.split(jax.random.fold_in(key, 29), 7)
    per_head_bias = jax.random.uniform(key_bias, (MAMBA_HEAD_COUNT,), jnp.float32, -13.0, -3.0)
    coarse_portion = jnp.clip(0.5 * jax.random.normal(key_rough, (MAMBA_HEAD_COUNT, SEQUENCE_LENGTH), jnp.float32), -2.0, 2.0)
    locations = jax.random.randint(key_location, (pulse_count,), 0, SEQUENCE_LENGTH)
    hit_flags = jnp.any(jnp.arange(SEQUENCE_LENGTH)[None, :] == locations[:, None], axis=0)
    pulse_raise = jax.random.uniform(key_raise, (MAMBA_HEAD_COUNT, 1), jnp.float32, -0.8, 0.2)
    steady_flags = jax.random.randint(key_steady, (MAMBA_HEAD_COUNT,), 0, 2) == 1
    steady_bias = jax.random.uniform(key_steady_bias, (MAMBA_HEAD_COUNT,), jnp.float32, -13.0, -9.0)
    steady_target = jax.random.uniform(key_target, (MAMBA_HEAD_COUNT, 1), jnp.float32, -6.6, -5.6)
    per_head_bias = jnp.where(steady_flags, steady_bias, per_head_bias)
    pulsed_rates = jnp.where(hit_flags[None, :], pulse_raise - per_head_bias[:, None], coarse_portion)
    steady_rates = steady_target - per_head_bias[:, None] + coarse_portion
    unshaped_rates = jnp.where(steady_flags[:, None], steady_rates, pulsed_rates)
    return (per_head_bias, unshaped_rates)


def draw_dt_raw(key, part):
    return rate_pieces(key)[1]


def draw_dt_bias(key, part):
    return rate_pieces(key)[0]


def drawn_pair(key):
    key_query, key_key = jax.random.split(jax.random.fold_in(key, 41), 2)
    query_shape = (SEQUENCE_LENGTH, QUERY_HEADS, KEY_DIM)
    key_shape = (SEQUENCE_LENGTH, KEY_HEADS, KEY_DIM)
    query_part = jnp.clip(2.5 * jax.random.normal(key_query, query_shape, jnp.float32), -10.0, 10.0)
    key_part = jnp.clip(jax.random.normal(key_key, key_shape, jnp.float32), -6.0, 6.0)
    return (query_part.reshape(SEQUENCE_LENGTH, -1), key_part.reshape(SEQUENCE_LENGTH, -1))


def draw_queries(key, part):
    return drawn_pair(key)[0].astype(jnp.bfloat16)


def draw_keys(key, part):
    return drawn_pair(key)[1].astype(jnp.bfloat16)


def shard_levels(rng, shape, cuts, smallest, largest):
    factor_of = 1.0
    for dim, shards_of in cuts:
        draws = jax.random.uniform(jax.random.fold_in(jax.random.fold_in(rng, 6), dim), (shards_of,), jnp.float32, smallest / len(cuts), largest / len(cuts))
        factor_of = factor_of * jnp.repeat(jnp.exp(draws), shape[dim] // shards_of).reshape((-1,) + (1,) * (len(shape) - 1 - dim))
    return factor_of


def centred(key, extent, width, bound, cuts=(), dtype=jnp.bfloat16):
    factor_of = shard_levels(key, extent, cuts, -0.22, 0.18) if cuts else 1.0
    values = jax.random.normal(key, extent, jnp.float32) * width * factor_of
    return jnp.minimum(jnp.maximum(values, -bound), bound).astype(dtype)


def setup_inputs(seed: int = 0, part: int = 0) -> dict:
    arg_keys = jax.random.split(jax.random.key(seed), 13)
    part_splits = jax.random.split(jax.random.fold_in(arg_keys[12], part), 13)
    return {
        "xbc": centred(part_splits[0], (SEQUENCE_LENGTH, MAMBA_HEAD_COUNT * SSM_HEAD_DIM + 2 * SSM_GROUPS * SSM_STATE), 1.0, 6.0, ((0, 16), (1, 8))),
        "gate_in": centred(part_splits[1], (SEQUENCE_LENGTH, MAMBA_HEAD_COUNT * SSM_HEAD_DIM), 1.0, 6.0, ((0, 16), (1, 8))),
        "dt_raw": draw_dt_raw(jax.random.fold_in(jax.random.fold_in(arg_keys[12], part), 71), part),
        "dt_bias": draw_dt_bias(jax.random.fold_in(jax.random.fold_in(arg_keys[12], part), 71), part),
        "a_log": jnp.clip(-0.7 + 0.7 * jax.random.uniform(arg_keys[4], (MAMBA_HEAD_COUNT,), jnp.float32) ** shard_levels(arg_keys[4], (MAMBA_HEAD_COUNT,), ((0, 8),), -0.2, 0.2), -0.7, 0.0),
        "conv_weight": centred(arg_keys[5], (CONV_WIDTH, MAMBA_HEAD_COUNT * SSM_HEAD_DIM + 2 * SSM_GROUPS * SSM_STATE), CONV_WIDTH ** -0.5, 3.0, ((1, 8),), jnp.float32),
        "conv_bias": centred(arg_keys[6], (MAMBA_HEAD_COUNT * SSM_HEAD_DIM + 2 * SSM_GROUPS * SSM_STATE,), 0.5, 3.0, ((0, 8),), jnp.float32),
        "skip_weight": jnp.clip(0.5 + 1.0 * jax.random.uniform(arg_keys[7], (MAMBA_HEAD_COUNT,), jnp.float32) ** shard_levels(arg_keys[7], (MAMBA_HEAD_COUNT,), ((0, 8),), -0.2, 0.2), 0.5, 1.5),
        "norm_gain": jnp.clip(1.0 + 0.1 * jax.random.normal(arg_keys[8], (MAMBA_HEAD_COUNT * SSM_HEAD_DIM,), jnp.float32), 0.5, 1.5),
        "queries": draw_queries(jax.random.fold_in(jax.random.fold_in(arg_keys[12], part), 71), part),
        "keys": draw_keys(jax.random.fold_in(jax.random.fold_in(arg_keys[12], part), 71), part),
        "values": centred(part_splits[11], (SEQUENCE_LENGTH, KEY_HEADS * KEY_DIM), 1.0, 6.0, ((0, 16), (1, 8))),
    }


eps = 1e-05
highest = lax.Precision.HIGHEST

def conv_section(xbc, conv_weight, conv_bias):
    taps_count = conv_weight.shape[0]
    row_count = xbc.shape[0]
    padded = jnp.concatenate([jnp.zeros((taps_count - 1, xbc.shape[1]), jnp.float32), xbc.astype(jnp.float32)], axis=0)
    running = jnp.zeros((row_count, xbc.shape[1]), jnp.float32) + conv_bias[None, :]
    for offset in range(taps_count):
        running = running + conv_weight[offset][None, :] * padded[offset:offset + row_count]
    return jax.nn.silu(running).astype(jnp.bfloat16)

def mamba_mixer(xbc, gate_in, dt_raw, dt_bias, a_log, conv_weight, conv_bias, skip_weight, norm_gain):
    per_group = MAMBA_HEAD_COUNT // SSM_GROUPS
    head_cols = MAMBA_HEAD_COUNT // N_TP * SSM_HEAD_DIM
    group_cols = SSM_GROUPS // N_TP * SSM_STATE
    conv_out = conv_section(xbc, conv_weight, conv_bias).reshape(SEQUENCE_LENGTH, N_TP, head_cols + 2 * group_cols)
    inputs = conv_out[:, :, :head_cols].reshape(SEQUENCE_LENGTH, MAMBA_HEAD_COUNT, SSM_HEAD_DIM)
    b_heads = jnp.repeat(conv_out[:, :, head_cols:head_cols + group_cols].reshape(SEQUENCE_LENGTH, SSM_GROUPS, SSM_STATE), per_group, axis=1)
    c_heads = jnp.repeat(conv_out[:, :, head_cols + group_cols:].reshape(SEQUENCE_LENGTH, SSM_GROUPS, SSM_STATE), per_group, axis=1)
    dt_step = jax.nn.softplus(dt_raw + dt_bias[:, None])
    log_decay = -dt_step * jnp.exp(a_log)[:, None]
    span_count = SEQUENCE_LENGTH // SPAN_LEN

    def by_span(array):
        return array.reshape((span_count, SPAN_LEN) + array.shape[1:])

    def by_span_heads(array):
        return array.reshape(MAMBA_HEAD_COUNT, span_count, SPAN_LEN).transpose(1, 0, 2)
    causal = jnp.arange(SPAN_LEN)[:, None] >= jnp.arange(SPAN_LEN)[None, :]

    def span_step(carried, pieces):
        x_span, b_span, c_span, dt_span, decay_span = pieces
        cumulative = jnp.cumsum(decay_span, axis=1)
        decay_gaps = cumulative[:, :, None] - cumulative[:, None, :]
        decay_matrix = jnp.where(causal[None], jnp.exp(jnp.where(causal[None], decay_gaps, 0.0)), 0.0)
        products = jnp.einsum('thn,shn->hts', c_span.astype(jnp.float32), b_span.astype(jnp.float32), precision=highest)
        mixing = (products * decay_matrix * dt_span[:, None, :]).astype(jnp.bfloat16)
        within_block = jnp.einsum('hts,shp->thp', mixing.astype(jnp.float32), x_span.astype(jnp.float32), precision=highest)
        tail_weight = dt_span * jnp.exp(cumulative[:, -1:] - cumulative)
        weighted = (x_span.astype(jnp.float32) * tail_weight.T[:, :, None]).astype(jnp.bfloat16)
        block_state = jnp.einsum('shn,shp->hpn', b_span.astype(jnp.float32), weighted.astype(jnp.float32), precision=highest)
        from_state = jnp.einsum('thn,hpn->thp', c_span.astype(jnp.float32), carried, precision=highest) * jnp.exp(cumulative).T[:, :, None]
        outputs = within_block + from_state + skip_weight[None, :, None] * x_span.astype(jnp.float32)
        carried = jnp.exp(cumulative[:, -1])[:, None, None] * carried + block_state
        return (carried, outputs)
    pieces = (by_span(inputs), by_span(b_heads), by_span(c_heads), by_span_heads(dt_step), by_span_heads(log_decay))
    final_state, outputs = lax.scan(span_step, jnp.zeros((MAMBA_HEAD_COUNT, SSM_HEAD_DIM, SSM_STATE), jnp.float32), pieces)
    mixer = outputs.reshape(SEQUENCE_LENGTH, MAMBA_HEAD_COUNT * SSM_HEAD_DIM) * jax.nn.silu(gate_in.astype(jnp.float32))
    grouped = mixer.reshape(SEQUENCE_LENGTH, SSM_GROUPS, -1)
    norm_scale = lax.rsqrt(lax.optimization_barrier(jnp.mean(grouped * grouped, axis=-1, keepdims=True)) + eps)
    return ((grouped * norm_scale).reshape(SEQUENCE_LENGTH, -1) * norm_gain[None, :]).astype(jnp.bfloat16)

def attention(queries, keys, values):
    repeat_count = QUERY_HEADS // KEY_HEADS
    score_scale = 1.0 / math.sqrt(KEY_DIM)
    query_heads = queries.reshape(SEQUENCE_LENGTH, QUERY_HEADS, KEY_DIM).transpose(1, 0, 2)
    key_heads = jnp.repeat(keys.reshape(SEQUENCE_LENGTH, KEY_HEADS, KEY_DIM).transpose(1, 0, 2), repeat_count, axis=0)
    value_heads = jnp.repeat(values.reshape(SEQUENCE_LENGTH, KEY_HEADS, KEY_DIM).transpose(1, 0, 2), repeat_count, axis=0)
    causal = jnp.arange(SEQUENCE_LENGTH)[:, None] >= jnp.arange(SEQUENCE_LENGTH)[None, :]

    def one_head(pieces):
        query_rows, key_rows, value_rows = pieces
        scores = jnp.dot(query_rows, key_rows.T, preferred_element_type=jnp.float32) * score_scale
        row_top = lax.optimization_barrier(jnp.max(jnp.where(causal, scores, -1e+30), axis=1, keepdims=True))
        weights = jnp.where(causal, jnp.exp(scores - row_top), 0.0)
        row_total = lax.optimization_barrier(jnp.sum(weights, axis=1, keepdims=True))
        return jnp.dot(weights.astype(jnp.bfloat16), value_rows, preferred_element_type=jnp.float32) / row_total
    heads_out = lax.map(one_head, (query_heads, key_heads, value_heads))
    return heads_out.transpose(1, 0, 2).reshape(SEQUENCE_LENGTH, -1).astype(jnp.bfloat16)

def reference(xbc, gate_in, dt_raw, dt_bias, a_log, conv_weight, conv_bias, skip_weight, norm_gain, queries, keys, values):
    mamba_out = mamba_mixer(xbc, gate_in, dt_raw, dt_bias, a_log, conv_weight, conv_bias, skip_weight, norm_gain)
    attn_out = attention(queries, keys, values)
    return (mamba_out, attn_out)
```

```python
import functools
import math

import jax
import jax.numpy as jnp
from jax import lax
from jax.experimental import pallas as pl
from jax.experimental.pallas import tpu as pltpu
from jax.sharding import PartitionSpec as P


HEAD_DIM = 64
STATE = 256
SPAN = 128
KEY_DIM = 128
HEADS = 16
QHEADS = 8
RING = 8
HALO = 8
CHANNELS = HEADS * HEAD_DIM
ROW_KV = 128
ROW_OTHER = 256
ROW_DECAY = 384
ROWS = 392
EPS = 1e-05
NEG = -1e30

f32 = jnp.float32
bf16 = jnp.bfloat16


def dot(a, b, dims, precision=None):
    return lax.dot_general(a, b, (dims, ((), ())), precision=precision, preferred_element_type=f32)


def pair_tile(columns, pair):
    lane = lax.broadcasted_iota(jnp.int32, (SPAN, 128), 1)
    return jnp.where(
        lane < HEAD_DIM, columns[:, 2 * pair : 2 * pair + 1], columns[:, 2 * pair + 1 : 2 * pair + 2]
    )


def front_kernel(
    xbc_ref, rim_ref, dt_raw_ref, dt_bias_ref, a_log_ref, cw_ref, cb_ref, keys_ref, values_ref, other_ref,
    send_ref, conv_ref, rows_ref, ext_ref,
):
    ext_ref[0:HALO, :] = rim_ref[...].astype(f32)
    ext_ref[HALO:, :] = xbc_ref[...].astype(f32)
    for col in range(0, CHANNELS + 2 * STATE, 256):
        cols = slice(col, col + 256)
        running = jnp.broadcast_to(cb_ref[:, cols], (SPAN, 256))
        for tap in range(4):
            running = running + cw_ref[tap : tap + 1, cols] * ext_ref[HALO - 3 + tap : HALO - 3 + tap + SPAN, cols]
        conv_ref[:, cols] = (running / (1.0 + jnp.exp(-running))).astype(bf16)
    raw = dt_raw_ref[...] + dt_bias_ref[...]
    dt_step = jnp.maximum(raw, 0.0) + jnp.log1p(jnp.exp(-jnp.abs(raw)))
    log_decay = -dt_step * jnp.exp(a_log_ref[...])
    earlier = (
        lax.broadcasted_iota(jnp.int32, (SPAN, SPAN), 0) <= lax.broadcasted_iota(jnp.int32, (SPAN, SPAN), 1)
    ).astype(f32)
    cum = dot(log_decay, earlier, ((1,), (0,)), lax.Precision.HIGHEST)
    last = cum[:, SPAN - 1 : SPAN]
    tail = dt_step * jnp.exp(last - cum)
    rows_ref[0:HEADS, :] = dt_step
    rows_ref[HEADS:, :] = cum
    tail_columns = jnp.transpose(jnp.concatenate([tail] * (SPAN // HEADS), axis=0))
    b_rows = conv_ref[:, CHANNELS : CHANNELS + STATE]
    total = jnp.broadcast_to(jnp.exp(last), (HEADS, STATE))
    total_hi = total.astype(bf16).astype(f32)
    total_lo = total - total_hi
    row = lax.broadcasted_iota(jnp.int32, (8, STATE), 0)
    for pair in range(RING):
        cols = slice(128 * pair, 128 * pair + 128)
        weighted = (conv_ref[:, cols].astype(f32) * pair_tile(tail_columns, pair)).astype(bf16)
        send_ref[pair, 0:128, :] = dot(weighted, b_rows, ((0,), (0,))).astype(bf16)
        send_ref[pair, ROW_KV:ROW_OTHER, 0:128] = keys_ref[...]
        send_ref[pair, ROW_KV:ROW_OTHER, 128:256] = values_ref[...]
        send_ref[pair, ROW_OTHER:ROW_DECAY, :] = other_ref[...]
        first, second = 2 * pair, 2 * pair + 1
        decays = jnp.where(row == 0, total_hi[first : first + 1], total_lo[first : first + 1])
        decays = jnp.where(row == 2, total_hi[second : second + 1], decays)
        decays = jnp.where(row >= 3, total_lo[second : second + 1], decays)
        send_ref[pair, ROW_DECAY:ROWS, :] = decays.astype(bf16)


def advance(state, got_ref, block):
    decays = got_ref[block, ROW_DECAY:ROWS, :].astype(f32)
    upper = state[0:HEAD_DIM] * (decays[0:1] + decays[1:2])
    lower = state[HEAD_DIM:] * (decays[2:3] + decays[3:4])
    return jnp.concatenate([upper, lower], axis=0) + got_ref[block, 0:128, :].astype(f32)


def total_kernel(got_ref, out_ref):
    state = got_ref[0, 0:128, :].astype(f32)
    for block in range(1, RING):
        state = advance(state, got_ref, block)
    out_ref[...] = state.astype(bf16)


def entry_kernel(got_ref, first_ref, out_ref):
    state = first_ref[...].astype(f32)
    for block in range(RING):
        out_ref[block] = state.astype(bf16)
        if block < RING - 1:
            state = advance(state, got_ref, block)


def within_kernel(conv_ref, rows_ref, skip_ref, out_ref):
    b_rows = conv_ref[:, CHANNELS : CHANNELS + STATE]
    c_rows = conv_ref[:, CHANNELS + STATE :]
    products = dot(c_rows, b_rows, ((1,), (1,)))
    causal = lax.broadcasted_iota(jnp.int32, (SPAN, SPAN), 0) >= lax.broadcasted_iota(jnp.int32, (SPAN, SPAN), 1)
    products = jnp.where(causal, products, 0.0)
    cum = rows_ref[HEADS:, :]
    cum_columns = jnp.transpose(jnp.concatenate([cum] * (SPAN // HEADS), axis=0))
    lane = lax.broadcasted_iota(jnp.int32, (SPAN, 128), 1)
    for pair in range(HEADS // 2):
        x_pair = conv_ref[:, 128 * pair : 128 * pair + 128]
        parts = []
        for head in (2 * pair, 2 * pair + 1):
            gaps = cum_columns[:, head : head + 1] - cum[head : head + 1, :]
            decay = jnp.exp(jnp.where(causal, gaps, 0.0))
            mixing = (products * decay * rows_ref[head : head + 1, :]).astype(bf16)
            parts.append(dot(mixing, x_pair, ((1,), (0,))))
        out_ref[:, 128 * pair : 128 * pair + 128] = (
            jnp.where(lane < HEAD_DIM, parts[0], parts[1])
            + skip_ref[:, 128 * pair : 128 * pair + 128] * x_pair.astype(f32)
        )


def attention_kernel(place_ref, got_ref, queries_ref, out_ref, bias_ref, keys_ref, values_ref):
    ring = place_ref[0]
    turn = place_ref[1]
    half = RING * SPAN
    for block in range(RING):
        rows = slice(SPAN * block, SPAN * block + SPAN)
        keys_ref[rows, :] = got_ref[block, ROW_OTHER:ROW_DECAY, 0:128]
        values_ref[rows, :] = got_ref[block, ROW_OTHER:ROW_DECAY, 128:256]
        rows = slice(half + SPAN * block, half + SPAN * block + SPAN)
        keys_ref[rows, :] = got_ref[block, ROW_KV:ROW_OTHER, 0:128]
        values_ref[rows, :] = got_ref[block, ROW_KV:ROW_OTHER, 128:256]
    key_pos = lax.broadcasted_iota(jnp.int32, (SPAN, 2 * half), 1) - half
    query_pos = lax.broadcasted_iota(jnp.int32, (SPAN, 2 * half), 0) + turn * SPAN
    seen = (key_pos <= query_pos) & ((key_pos >= 0) | (ring > 0))
    bias_ref[...] = jnp.where(seen, 0.0, NEG)
    scale = 1.0 / math.sqrt(KEY_DIM)
    for head in range(QHEADS):
        cols = slice(KEY_DIM * head, KEY_DIM * head + KEY_DIM)
        scores = dot(queries_ref[:, cols], keys_ref[...], ((1,), (1,))) * scale + bias_ref[...]
        best = jnp.max(scores, axis=1, keepdims=True)
        weights = jnp.exp(scores - best)
        total = jnp.sum(weights, axis=1, keepdims=True)
        mixed = dot(weights.astype(bf16), values_ref[...], ((1,), (0,)))
        out_ref[:, cols] = (mixed / total).astype(bf16)


def finish_kernel(states_ref, conv_ref, rows_ref, within_ref, gate_ref, gain_ref, out_ref, y_ref):
    c_rows = conv_ref[:, CHANNELS + STATE :]
    cum = rows_ref[HEADS:, :]
    grow = jnp.transpose(jnp.concatenate([jnp.exp(cum)] * (SPAN // HEADS), axis=0))
    squares = jnp.zeros((SPAN, 128), f32)
    for pair in range(HEADS // 2):
        cols = slice(128 * pair, 128 * pair + 128)
        carried = dot(c_rows, states_ref[pair], ((1,), (1,))) * pair_tile(grow, pair)
        gate = gate_ref[:, cols].astype(f32)
        value = (within_ref[:, cols] + carried) * (gate / (1.0 + jnp.exp(-gate)))
        y_ref[:, cols] = value
        squares = squares + value * value
    scale = lax.rsqrt(jnp.sum(squares, axis=1, keepdims=True) / CHANNELS + EPS)
    out_ref[...] = (y_ref[...] * scale * gain_ref[...]).astype(bf16)


def call(kernel, out_shape, scratch=(), scalars=0, flops=10**7, moved=2 * 10**6):
    vmem = pl.BlockSpec(memory_space=pltpu.VMEM)

    def run(*operands):
        specs = [pl.BlockSpec(memory_space=pltpu.SMEM)] * scalars + [vmem] * (len(operands) - scalars)
        return pl.pallas_call(
            kernel,
            out_shape=out_shape,
            in_specs=specs,
            out_specs=jax.tree.map(lambda _: vmem, out_shape),
            scratch_shapes=list(scratch),
            cost_estimate=pl.CostEstimate(flops=flops, bytes_accessed=moved, transcendentals=0),
        )(*operands)

    return run


def shards(
    rings, xbc, gate_in, dt_raw, dt_bias, a_log, conv_weight, conv_bias, skip_weight, norm_gain, queries, keys, values
):
    count = rings * RING
    groups = [[ring * RING + turn for turn in range(RING)] for ring in range(rings)]
    crossing = [(turn, RING + turn) for turn in range(RING)]
    rim = lax.ppermute(xbc[SPAN - HALO :], "ctx", [(i, i + 1) for i in range(count - 1)])
    other = lax.ppermute(jnp.concatenate([keys, values], axis=1), "ctx", crossing)
    send, conv, rows = call(
        front_kernel,
        (
            jax.ShapeDtypeStruct((RING, ROWS, STATE), bf16),
            jax.ShapeDtypeStruct((SPAN, CHANNELS + 2 * STATE), bf16),
            jax.ShapeDtypeStruct((2 * HEADS, SPAN), f32),
        ),
        scratch=[pltpu.VMEM((SPAN + HALO, CHANNELS + 2 * STATE), f32)],
    )(
        xbc, rim, dt_raw, dt_bias[:, None], a_log[:, None], conv_weight, conv_bias[None, :], keys, values, other
    )
    got = lax.all_to_all(send, "ctx", 0, 0, axis_index_groups=groups, tiled=True)
    ring_total = call(total_kernel, jax.ShapeDtypeStruct((128, STATE), bf16))(got)
    first = lax.ppermute(ring_total, "ctx", crossing)
    index = lax.axis_index("ctx")
    place = jnp.stack([index // RING, index % RING]).astype(jnp.int32)
    attn_out = call(
        attention_kernel,
        jax.ShapeDtypeStruct((SPAN, QHEADS * KEY_DIM), bf16),
        scratch=[
            pltpu.VMEM((SPAN, 2 * RING * SPAN), f32),
            pltpu.VMEM((2 * RING * SPAN, KEY_DIM), bf16),
            pltpu.VMEM((2 * RING * SPAN, KEY_DIM), bf16),
        ],
        scalars=1,
        flops=10**9,
    )(place, got, queries)
    within = call(within_kernel, jax.ShapeDtypeStruct((SPAN, CHANNELS), f32), flops=10**8)(
        conv, rows, jnp.repeat(skip_weight, HEAD_DIM)[None, :]
    )
    first, attn_out, within = lax.optimization_barrier((first, attn_out, within))
    entries = call(entry_kernel, jax.ShapeDtypeStruct((RING, 128, STATE), bf16))(got, first)
    states = lax.all_to_all(entries, "ctx", 0, 0, axis_index_groups=groups, tiled=True)
    mamba_out = call(
        finish_kernel,
        jax.ShapeDtypeStruct((SPAN, CHANNELS), bf16),
        scratch=[pltpu.VMEM((SPAN, CHANNELS), f32)],
    )(states, conv, rows, within, gate_in, norm_gain[None, :])
    return mamba_out, attn_out


def solution(mesh):
    rows = P(("dp", "ctx"), "tp")
    placed = (
        rows,
        rows,
        P("tp", ("dp", "ctx")),
        P(("dp", "tp")),
        P("tp"),
        P(None, "tp"),
        P("tp"),
        P("tp"),
        P("tp"),
        rows,
        rows,
        rows,
    )
    return jax.shard_map(
        functools.partial(shards, mesh.shape["ctx"] // RING),
        mesh=mesh,
        in_specs=placed,
        out_specs=(rows, rows),
        check_vma=False,
    )
```
